256 devices in a mesh: view: 32 (over z_lo, y, x), slab: 8 (over z_hi, core).
Axes of the slice: x: 4, y: 4, z: 8 (z_hi: 4, z_lo: 2; z = z_hi * 2 + z_lo), core: 2. Of those that a mesh axis runs over, the one named last changes fastest.
Arguments:
- tiles: bfloat16 [32, 8, 64, 128, 128], P('view', 'slab'), may hold values from 0 to 0.36621094
- tile_bin: int32 [32, 8, 64], P('view', 'slab'), may hold values from 0 to 7
- tile_vox: int32 [32, 8, 64], P('view', 'slab'), may hold values from 0 to 7
- tile_count: int32 [32, 8], P('view', 'slab'), may hold values from 8 to 64, as said below
- subset: int32 [256], P('view'), may hold values from 0 to 1, as said below
- pairs: int32 [2, 32768], P(None, 'view'), may hold values from 0 to 3359
- measured: float32 [32768, 128], P('view'), may hold values from 0.2 to 5
- background: float32 [32768], P('view'), may hold values from 0.3 to 3
- image: float32 [8192, 128], P('slab'), may hold values from 0.5 to 2
- efficiency: float32 [3360], P('view'), may hold values from 0.5 to 1.5
Outputs:
- image_out: float32 [8192, 128], P('slab')
- efficiency_out: float32 [3360], P('view')
The draws below stay inside these ranges and needn't reach their ends.
Inputs may be any that keep to these rules, and one draw needn't show every extreme that they name: tiles at positions tile_count or later in a list are not part of the projector; some list is full in every draw. The 8 tile rows of bins of each view shard hold exactly 4 rows of each subset.
All inputs are finite; a program needn't handle non-finite values.
Results may differ from the reference program's by a relative error of at most 0.00079.
Values may be sent and summed in bfloat16 or wider, within the bound.
A program may use at most 64 MiB of HBM per device.

```python
import math
import jax
import jax.numpy as jnp
from jax import lax

TB = 128
NT = 64
BB_DEV = 8
VB_DEV = 8
FRAMES = 128
SUBSETS = 2
NC = 3360
BINS = 32768
VOX = 8192
N_VIEW = 32
N_SLAB = 8


def draw_tile_count(key, part):
    exponent = jax.random.randint(key, (N_VIEW, N_SLAB), 0, 4, dtype=jnp.int32)
    counts = jnp.maximum(NT // jnp.power(2, exponent), 1)
    spot = jax.random.randint(jax.random.fold_in(key, 1), (), 0, N_VIEW * N_SLAB, dtype=jnp.int32)
    flat = counts.reshape(-1)
    flat = jnp.where(jnp.arange(N_VIEW * N_SLAB, dtype=jnp.int32) == spot, NT, flat)
    return flat.reshape(N_VIEW, N_SLAB).astype(jnp.int32)


def shard_order(single_key):
    return jax.random.permutation(single_key, BB_DEV)


def draw_subset(key, part):
    shard_keys = jax.random.split(jax.random.fold_in(key, 7), N_VIEW)
    orders = jax.vmap(shard_order)(shard_keys)
    return (orders % SUBSETS).reshape(N_VIEW * BB_DEV).astype(jnp.int32)


def draw_tiles(key, part):
    mean_entry = BB_DEV / (NT * TB * N_SLAB)
    spread = 2.0
    edge = 4.0
    normal = jax.random.normal(jax.random.fold_in(key, 11), (N_VIEW, N_SLAB, NT, TB, TB), jnp.float32)
    normal = jnp.clip(normal, -edge, edge)
    values = mean_entry * jnp.exp(spread * normal - spread)
    return values.astype(jnp.bfloat16)


def place_ends(values, stream_key, least, largest):
    place = [jax.random.randint(jax.random.fold_in(stream_key, axis), (), 0, length) for axis, length in enumerate(values.shape)]
    widest = values.shape.index(max(values.shape))
    neighbour = place[:widest] + [(place[widest] + 1) % values.shape[widest]] + place[widest + 1:]
    return values.at[tuple(place)].set(least).at[tuple(neighbour)].set(largest)


def level_of(rng, extent, cuts, least, top_value):
    def one(dim, parts):
        draws = jax.random.uniform(jax.random.fold_in(jax.random.fold_in(rng, 6), dim), (parts,), jnp.float32, least / len(cuts), top_value / len(cuts))
        return jnp.repeat(jnp.exp(draws), extent[dim] // parts).reshape((-1,) + (1,) * (len(extent) - dim - 1))

    level = one(*cuts[0])
    for cut in cuts[1:]:
        level = level * one(*cut)
    return level


def setup_inputs(seed: int = 0) -> dict:
    key_of = jax.random.split(jax.random.key(seed), 11)
    return {
        "tiles": draw_tiles(jax.random.fold_in(key_of[10], 71), 0),
        "tile_bin": place_ends(jax.random.randint(key_of[1], (N_VIEW, N_SLAB, NT), 0, BB_DEV), jax.random.fold_in(key_of[1], 1), 0, BB_DEV - 1).astype(jnp.int32),
        "tile_vox": place_ends(jax.random.randint(key_of[2], (N_VIEW, N_SLAB, NT), 0, VB_DEV), jax.random.fold_in(key_of[2], 1), 0, VB_DEV - 1).astype(jnp.int32),
        "tile_count": draw_tile_count(jax.random.fold_in(key_of[10], 71), 0),
        "subset": draw_subset(jax.random.fold_in(key_of[10], 71), 0),
        "pairs": place_ends(jax.random.randint(key_of[5], (2, BINS), 0, NC), jax.random.fold_in(key_of[5], 1), 0, NC - 1).astype(jnp.int32),
        "measured": jnp.clip(jnp.exp(math.log(5.0) - 3.218876 * jax.random.uniform(key_of[6], (BINS, FRAMES), jnp.float32) ** level_of(key_of[6], (BINS, FRAMES), ((0, 32),), -0.2, 0.2)), 0.2, 5.0),
        "background": jnp.clip(jnp.exp(math.log(3.0) - 2.3025851 * jax.random.uniform(key_of[7], (BINS,), jnp.float32) ** level_of(key_of[7], (BINS,), ((0, 32),), -0.2, 0.2)), 0.3, 3.0),
        "image": jnp.clip(jnp.exp(math.log(2.0) - 1.3862944 * jax.random.uniform(key_of[8], (VOX, FRAMES), jnp.float32) ** level_of(key_of[8], (VOX, FRAMES), ((0, 8),), -0.2, 0.2)), 0.5, 2.0),
        "efficiency": jnp.clip(1.0 + 0.1 * jax.random.normal(key_of[9], (NC,), jnp.float32), 0.5, 1.5),
    }


SMOOTH = 0.1
FAN_OFFSET = 1.0


def forward_pass(tiles, tile_bin, tile_vox, active, image_half):
    slab_images = image_half.reshape(N_SLAB, VB_DEV, TB, FRAMES).astype(jnp.float32)

    def one_pair(blocks, bin_ids, vox_ids, weights, slab_image):
        picked = slab_image[vox_ids]
        partial_value = jnp.einsum("tij,tjf->tif", blocks.astype(jnp.float32), picked) * weights[:, None, None]
        return jax.ops.segment_sum(partial_value, bin_ids, num_segments=BB_DEV)

    def one_view(pieces):
        blocks, bin_ids, vox_ids, weights = pieces
        return jnp.sum(jax.vmap(one_pair)(blocks, bin_ids, vox_ids, weights, slab_images), axis=0)

    summed = lax.map(one_view, (tiles, tile_bin, tile_vox, active))
    return summed.reshape(BINS, FRAMES)


def by_slab(array_in):
    return jnp.swapaxes(array_in, 0, 1)


def back_pass(tiles, tile_bin, tile_vox, active, ratios, weights_half):
    view_ratio = ratios.reshape(N_VIEW, BB_DEV, TB, FRAMES).astype(jnp.float32)
    view_weight = weights_half.reshape(N_VIEW, BB_DEV, TB).astype(jnp.float32)

    def one_slab(pieces):
        blocks, bin_ids, vox_ids, weights = pieces

        def add_view(totals, per_view):
            view_tiles, bins_here, voxels_here, view_active, view_rat, view_wgt = per_view
            view_tiles = view_tiles.astype(jnp.float32)
            image_part = jnp.einsum("tij,tif->tjf", view_tiles, view_rat[bins_here]) * view_active[:, None, None]
            sens_part = jnp.einsum("tij,ti->tj", view_tiles, view_wgt[bins_here]) * view_active[:, None]
            first = totals[0] + jax.ops.segment_sum(image_part, voxels_here, num_segments=VB_DEV)
            second = totals[1] + jax.ops.segment_sum(sens_part, voxels_here, num_segments=VB_DEV)
            return (first, second), None

        start_sums = (jnp.zeros((VB_DEV, TB, FRAMES), jnp.float32), jnp.zeros((VB_DEV, TB), jnp.float32))
        result, unused = lax.scan(add_view, start_sums, (blocks, bin_ids, vox_ids, weights, view_ratio, view_weight))
        return result

    back_image, sensitivity = lax.map(one_slab, (by_slab(tiles), by_slab(tile_bin), by_slab(tile_vox), by_slab(active)))
    return back_image.reshape(VOX, FRAMES), sensitivity.reshape(VOX)


def reference(tiles, tile_bin, tile_vox, tile_count, subset, pairs, measured, background, image, efficiency):
    active = (jnp.arange(NT, dtype=jnp.int32)[None, None, :] < tile_count[:, :, None]).astype(jnp.float32)
    weight = efficiency[pairs[0]] * efficiency[pairs[1]]
    bin_subset = jnp.repeat(subset, TB)
    estimate = image
    for subset_index in range(SUBSETS):
        image_half = estimate.astype(jnp.bfloat16)
        forward = forward_pass(tiles, tile_bin, tile_vox, active, image_half)
        subset_weight = jnp.where(bin_subset == subset_index, weight, jnp.zeros_like(weight))
        ratios = (subset_weight[:, None] * measured / (weight[:, None] * forward + background[:, None])).astype(jnp.bfloat16)
        back_image, sensitivity = back_pass(tiles, tile_bin, tile_vox, active, ratios, subset_weight.astype(jnp.bfloat16))
        estimate = estimate * (back_image + SMOOTH) / (sensitivity[:, None] + SMOOTH)
    final = forward_pass(tiles, tile_bin, tile_vox, active, estimate.astype(jnp.bfloat16))
    expected = jnp.sum(weight[:, None] * final + background[:, None], axis=1)
    counted = jnp.sum(measured, axis=1)
    fan_counts = jax.ops.segment_sum(counted, pairs[0], num_segments=NC) + jax.ops.segment_sum(counted, pairs[1], num_segments=NC)
    fan_expected = jax.ops.segment_sum(expected, pairs[0], num_segments=NC) + jax.ops.segment_sum(expected, pairs[1], num_segments=NC)
    efficiency_out = efficiency * (fan_counts + FAN_OFFSET) / (fan_expected + FAN_OFFSET)
    return estimate, efficiency_out
```

```python
import jax
import jax.numpy as jnp
from jax import lax
from jax.experimental import pallas as pl
from jax.experimental.pallas import tpu as pltpu
from jax.sharding import PartitionSpec as P

SUBSETS = 2
SMOOTH = 0.1
FAN_OFFSET = 1.0
MESH = pl.DeviceIdType.MESH
F32 = jnp.float32
BF16 = jnp.bfloat16
VMEM = pltpu.VMEM
SMEM = pltpu.SMEM

NV = 32
NS = 8
TB = 128
NB = 8
BINS = 1024
HALF = BINS // SUBSETS
VOX = 1024
FR = 128
FPART = FR // NS
VQ = 4
VW = VOX // VQ
OWN = 105

NN = (((1,), (0,)), ((), ()))
NT = (((1,), (1,)), ((), ()))
TN = (((0,), (0,)), ((), ()))


def dot(a, b, dims):
    return lax.dot_general(a, b, dims, preferred_element_type=F32)


def pieces(x):
    hi = x.astype(BF16)
    rest = x - hi.astype(F32)
    mid = rest.astype(BF16)
    low = (rest - mid.astype(F32)).astype(BF16)
    return hi, mid, low


def fan(values, oh_hi, oh_lo):
    parts = [jnp.where(oh_hi > 0, jnp.broadcast_to(p.astype(F32), oh_hi.shape), 0.0) for p in pieces(values)]
    lhs = jnp.concatenate(parts, axis=0).astype(BF16)
    out = dot(lhs, oh_lo, NT)
    return out[0:NV] + out[NV : 2 * NV] + out[2 * NV : 3 * NV]


def prepare(
    tile_bin, tile_vox, tile_count, subset, tiles, pairs, measured, background, image, efficiency,
    a_ref, part_ref, meas_ref, back_ref, hi_ref, lo_ref, est_ref, eff_ref, counts_ref,
    acc, img_t, meas_t, pair_s,
):
    v = lax.axis_index("view")
    s = lax.axis_index("slab")
    spots = []
    seen = [jnp.int32(0), jnp.int32(0)]
    for row in range(NB):
        k = subset[row]
        spots.append(jnp.where(k == 0, seen[0], NB // SUBSETS + seen[1]))
        seen = [seen[0] + jnp.where(k == 0, 1, 0), seen[1] + jnp.where(k == 0, 0, 1)]

    def spot_of(row):
        out = spots[0]
        for i in range(1, NB):
            out = jnp.where(row == i, spots[i], out)
        return out

    acc[...] = jnp.zeros_like(acc)

    @pl.loop(0, tile_count[0])
    def _(t):
        p = spot_of(tile_bin[t])
        cols = pl.ds(pl.multiple_of(tile_vox[t] * TB, TB), TB)
        acc[p, :, cols] += tiles[t].astype(F32)

    for row in range(NB):
        a_ref[pl.ds(row * TB, TB), :] = acc[row].astype(BF16)
        lanes = pl.ds(pl.multiple_of(spots[row] * TB, TB), TB)
        meas_t[:, lanes] = measured[pl.ds(row * TB, TB), :].T
        back_ref[:, lanes] = background[:, pl.ds(row * TB, TB)]
        pair_s[:, lanes] = pairs[:, pl.ds(row * TB, TB)]
        img_t[:, pl.ds(row * TB, TB)] = image[pl.ds(row * TB, TB), :].T

    meas_ref[...] = meas_t[pl.ds(pl.multiple_of(s * FPART, FPART), FPART), :]
    est_ref[...] = img_t[
        pl.ds(pl.multiple_of((v // VQ) * FPART, FPART), FPART),
        pl.ds(pl.multiple_of(lax.rem(v, VQ) * VW, VW), VW),
    ]
    eff_ref[...] = jnp.zeros_like(eff_ref)
    eff_ref[0, :, 0:OWN] = efficiency[...]

    ends = jnp.concatenate([pair_s[0:1, :], pair_s[1:2, :]], axis=1)
    high = jnp.floor((ends.astype(F32) + 0.5) * (1.0 / OWN)).astype(jnp.int32)
    low = ends - high * OWN
    oh_hi = jnp.where(lax.broadcasted_iota(jnp.int32, (NV, 2 * BINS), 0) == high, 1.0, 0.0)
    oh_lo = jnp.where(lax.broadcasted_iota(jnp.int32, (TB, 2 * BINS), 0) == low, 1.0, 0.0).astype(BF16)
    hi_ref[...] = oh_hi
    lo_ref[...] = oh_lo

    counted = jnp.sum(meas_t[...], axis=0, keepdims=True)
    counts_ref[...] = fan(jnp.concatenate([counted, counted], axis=1), oh_hi, oh_lo)

    part = dot(img_t[...].astype(BF16), a_ref[0:HALF, :], NT)
    part_ref[...] = part.astype(BF16).reshape(NS, FPART, HALF)


def exchange(
    a_ref, part_ref, meas_ref, back_ref, hi_ref, lo_ref, est_ref, eff_ref, counts_ref,
    out_ref, gain_ref,
    table, fwd_send, fwd, rat, sens_send, sens, bck_send, bck, img_send, img,
    sum_send, sums, fin_send, fin, q_send, q_recv, fan_send, fan_recv,
    send_sem, recv_sem,
):
    v = lax.axis_index("view")
    s = lax.axis_index("slab")
    barrier = pltpu.get_barrier_semaphore()

    def view_peer(i):
        return lax.rem(v + i, NV)

    def slab_peer(i):
        return lax.rem(s + i, NS)

    @pl.loop(1, NV)
    def _(i):
        pl.semaphore_signal(barrier, inc=1, device_id=(view_peer(i), s), device_id_type=MESH)

    @pl.loop(1, NS)
    def _(i):
        pl.semaphore_signal(barrier, inc=1, device_id=(v, slab_peer(i)), device_id_type=MESH)

    pl.semaphore_wait(barrier, NV - 1 + NS - 1)

    def to_views(phase, source, target):
        @pl.loop(1, NV)
        def _(i):
            w = view_peer(i)
            pltpu.make_async_remote_copy(
                src_ref=source(w), dst_ref=target, send_sem=send_sem.at[phase], recv_sem=recv_sem.at[phase],
                device_id=(w, s), device_id_type=MESH,
            ).start()

    def to_slabs(phase, source, target):
        @pl.loop(1, NS)
        def _(i):
            w = slab_peer(i)
            pltpu.make_async_remote_copy(
                src_ref=source(w), dst_ref=target, send_sem=send_sem.at[phase], recv_sem=recv_sem.at[phase],
                device_id=(v, w), device_id_type=MESH,
            ).start()

    def await_all(sem, ref):
        pltpu.make_async_copy(ref, ref, sem).wait()

    def views_of(ref):
        return ref.at[pl.ds(0, NV - 1)]

    def slabs_of(ref):
        return ref.at[pl.ds(0, NS - 1)]

    sent = [(0, slabs_of(fwd.at[0])), (1, views_of(table))]
    fi = v // VQ
    vi = lax.rem(v, VQ)
    frames = pl.ds(pl.multiple_of(fi * FPART, FPART), FPART)
    slot = vi * NS + fi

    to_slabs(0, lambda w: part_ref.at[w], fwd.at[0, s])
    to_views(1, lambda w: eff_ref.at[0], table.at[v])
    fwd[0, s] = part_ref[s]
    table[v] = eff_ref[0]

    await_all(recv_sem.at[1], views_of(table))
    rows = table[...].reshape(NV, TB)
    oh_hi = hi_ref[...]
    oh_lo = lo_ref[...]
    cols = jnp.concatenate([p.astype(F32) for p in pieces(rows)], axis=0).astype(BF16)
    hi3 = jnp.concatenate([oh_hi, oh_hi, oh_hi], axis=0).astype(BF16)
    picked = dot(cols, hi3, TN)
    ends = jnp.sum(jnp.where(oh_lo > 0, picked, 0.0), axis=0, keepdims=True)
    weight = ends[:, 0:BINS] * ends[:, BINS : 2 * BINS]
    back = back_ref[...]

    phase = 2
    for k in range(SUBSETS):
        bins = slice(k * HALF, (k + 1) * HALF)
        w_k = weight[:, bins]
        fwd_phase = 0 if k == 0 else phase
        if k > 0:
            total = jnp.zeros((FR, HALF), F32)
            for q in range(VQ):
                quarter = img[q * NS : (q + 1) * NS].reshape(FR, VW)
                total = total + dot(quarter, a_ref[bins, q * VW : (q + 1) * VW], NT)
            fwd_send[...] = total.astype(BF16).reshape(NS, FPART, HALF)
            to_slabs(phase, lambda w: fwd_send.at[w], fwd.at[k, s])
            fwd[k, s] = fwd_send[s]
            sent.append((phase, slabs_of(fwd.at[k])))
            phase += 1
        await_all(recv_sem.at[fwd_phase], slabs_of(fwd.at[k]))
        summed = jnp.sum(fwd[k].astype(F32), axis=0)
        ratio = (w_k * meas_ref[:, bins]) / (w_k * summed + back[:, bins])
        rat[k, s] = ratio.astype(BF16)
        to_slabs(phase, lambda w: rat.at[k, s], rat.at[k, s])
        rat_phase = phase
        sent.append((rat_phase, slabs_of(rat.at[k])))
        phase += 1

        if k == 0:
            row = lax.broadcasted_iota(jnp.int32, (16, BINS), 0)
            half = lax.broadcasted_iota(jnp.int32, (16, BINS), 1) // HALF
            lhs = jnp.where(row == half, jnp.broadcast_to(weight, (16, BINS)), 0.0).astype(BF16)
            both = dot(lhs, a_ref[...], NN)
            for q in range(VQ):
                sens_send[q] = both[0:SUBSETS, q * VW : (q + 1) * VW]
            sens_phase = phase
            phase += 1
            to_views(sens_phase, lambda w: sens_send.at[lax.rem(w, VQ)], sens.at[v])
            sens[v] = sens_send[vi]
            sent.append((sens_phase, views_of(sens)))

        await_all(recv_sem.at[rat_phase], slabs_of(rat.at[k]))
        lhs = rat[k].reshape(FR, HALF)
        for q in range(VQ):
            bck_send[k, q] = dot(lhs, a_ref[bins, q * VW : (q + 1) * VW], NN).astype(BF16)
        to_views(
            phase,
            lambda w: bck_send.at[k, lax.rem(w, VQ), pl.ds(pl.multiple_of((w // VQ) * FPART, FPART), FPART), :],
            bck.at[k, v],
        )
        bck[k, v] = bck_send[k, vi, frames, :]
        bck_phase = phase
        sent.append((bck_phase, views_of(bck.at[k])))
        phase += 1

        if k == 0:
            await_all(recv_sem.at[sens_phase], views_of(sens))
            sens_sum = jnp.sum(sens[...], axis=0)
            est = est_ref[...]
        await_all(recv_sem.at[bck_phase], views_of(bck.at[k]))
        back_image = jnp.sum(bck[k].astype(F32), axis=0)
        est = est * (back_image + SMOOTH) / (sens_sum[k : k + 1, :] + SMOOTH)
        half_image = est.astype(BF16)
        if k < SUBSETS - 1:
            img_send[...] = half_image
            to_views(phase, lambda w: img_send, img.at[slot])
            img[slot] = half_image
            await_all(recv_sem.at[phase], views_of(img))
            sent.append((phase, views_of(img)))
            phase += 1

    part_sum = jnp.sum(half_image.astype(F32), axis=0, keepdims=True)
    sum_send[...] = part_sum
    sum_phase = phase
    to_views(sum_phase, lambda w: sum_send, sums.at[v])
    sums[v] = part_sum
    fin_send[...] = est
    fin_phase = phase + 1
    to_views(fin_phase, lambda w: fin_send, fin.at[slot])
    fin[slot] = est
    sent += [(sum_phase, views_of(sums)), (fin_phase, views_of(fin))]
    phase += 2

    await_all(recv_sem.at[sum_phase], views_of(sums))
    quarter = []
    for q in range(VQ):
        total = sums[q]
        for f in range(1, NS):
            total = total + sums[f * VQ + q]
        quarter.append(total)
    image_sum = jnp.concatenate(quarter, axis=1)
    row = lax.broadcasted_iota(jnp.int32, (16, VOX), 0)
    hi, mid, low = [jnp.broadcast_to(p.astype(F32), (16, VOX)) for p in pieces(image_sum)]
    lhs = jnp.where(row == 0, hi, jnp.where(row == 1, mid, jnp.where(row == 2, low, 0.0))).astype(BF16)
    bins_sum = jnp.sum(dot(lhs, a_ref[...], NT), axis=0, keepdims=True)
    q_send[...] = bins_sum
    to_slabs(phase, lambda w: q_send, q_recv.at[s])
    q_recv[s] = bins_sum
    await_all(recv_sem.at[phase], slabs_of(q_recv))
    sent.append((phase, slabs_of(q_recv)))
    phase += 1
    final = jnp.sum(q_recv[...], axis=0)
    expected = weight * final + FR * back
    fan_exp = fan(jnp.concatenate([expected, expected], axis=1), oh_hi, oh_lo)
    fan_send[:, 0:1, :] = counts_ref[...].reshape(NV, 1, TB)
    fan_send[:, 1:2, :] = fan_exp.reshape(NV, 1, TB)
    to_views(phase, lambda w: fan_send.at[w], fan_recv.at[v])
    fan_recv[v] = fan_send[v]

    await_all(recv_sem.at[fin_phase], views_of(fin))
    for q in range(VQ):
        out_ref[pl.ds(q * VW, VW), :] = fin[q * NS : (q + 1) * NS].reshape(FR, VW).T

    await_all(recv_sem.at[phase], views_of(fan_recv))
    totals = jnp.sum(fan_recv[...], axis=0)
    gain = eff_ref[0] * (totals[0:1, :] + FAN_OFFSET) / (totals[1:2, :] + FAN_OFFSET)
    gain_ref[...] = gain[:, 0:OWN]
    sent.append((phase, views_of(fan_recv)))
    for number, ref in sent:
        await_all(send_sem.at[number], ref)


PHASES = 13


def on_device(
    tiles, tile_bin, tile_vox, tile_count, subset, pairs, measured, background, image, efficiency
):
    smem = pl.BlockSpec(memory_space=SMEM)
    vmem = pl.BlockSpec(memory_space=VMEM)
    shape = jax.ShapeDtypeStruct
    prepared = pl.pallas_call(
        prepare,
        out_shape=(
            shape((BINS, VOX), BF16),
            shape((NS, FPART, HALF), BF16),
            shape((FPART, BINS), F32),
            shape((1, BINS), F32),
            shape((NV, 2 * BINS), F32),
            shape((TB, 2 * BINS), BF16),
            shape((FPART, VW), F32),
            shape((1, 1, TB), F32),
            shape((NV, TB), F32),
        ),
        in_specs=[smem] * 4 + [vmem] * 6,
        out_specs=(vmem,) * 9,
        scratch_shapes=[
            VMEM((NB, TB, VOX), F32),
            VMEM((FR, VOX), F32),
            VMEM((FR, BINS), F32),
            VMEM((2, BINS), jnp.int32),
        ],
        name="prepare",
    )(
        tile_bin.reshape(-1),
        tile_vox.reshape(-1),
        tile_count.reshape(-1),
        subset,
        tiles.reshape(tiles.shape[2:]),
        pairs,
        measured,
        background.reshape(1, BINS),
        image,
        efficiency.reshape(1, OWN),
    )
    image_out, gain = pl.pallas_call(
        exchange,
        out_shape=(shape((VOX, FR), F32), shape((1, OWN), F32)),
        in_specs=[vmem] * 9,
        out_specs=(vmem, vmem),
        scratch_shapes=[
            VMEM((NV, 1, TB), F32),
            VMEM((NS, FPART, HALF), BF16),
            VMEM((SUBSETS, NS, FPART, HALF), BF16),
            VMEM((SUBSETS, NS, FPART, HALF), BF16),
            VMEM((VQ, SUBSETS, VW), F32),
            VMEM((NV, SUBSETS, VW), F32),
            VMEM((SUBSETS, VQ, FR, VW), BF16),
            VMEM((SUBSETS, NV, FPART, VW), BF16),
            VMEM((FPART, VW), BF16),
            VMEM((NV, FPART, VW), BF16),
            VMEM((1, VW), F32),
            VMEM((NV, 1, VW), F32),
            VMEM((FPART, VW), F32),
            VMEM((NV, FPART, VW), F32),
            VMEM((1, BINS), F32),
            VMEM((NS, 1, BINS), F32),
            VMEM((NV, 2, TB), F32),
            VMEM((NV, 2, TB), F32),
            pltpu.SemaphoreType.DMA((PHASES,)),
            pltpu.SemaphoreType.DMA((PHASES,)),
        ],
        compiler_params=pltpu.CompilerParams(collective_id=0, has_side_effects=True),
        name="exchange",
    )(*prepared)
    return image_out, gain.reshape(OWN)


def solution(mesh):
    return jax.shard_map(
        on_device,
        mesh=mesh,
        in_specs=(
            P("view", "slab", None, None, None),
            P("view", "slab", None),
            P("view", "slab", None),
            P("view", "slab"),
            P("view"),
            P(None, "view"),
            P("view", None),
            P("view"),
            P("slab", None),
            P("view"),
        ),
        out_specs=(P("slab", None), P("view")),
        check_vma=False,
    )
```

```python
import jax
import jax.numpy as jnp
from jax import lax
from jax.experimental import pallas as pl
from jax.experimental.pallas import tpu as pltpu
from jax.sharding import PartitionSpec as P

SUBSETS = 2
SMOOTH = 0.1
FAN_OFFSET = 1.0
MESH = pl.DeviceIdType.MESH
F32 = jnp.float32
BF16 = jnp.bfloat16
VMEM = pltpu.VMEM
SMEM = pltpu.SMEM

NV = 32
NS = 8
TB = 128
NB = 8
BINS = 1024
HALF = BINS // SUBSETS
VOX = 1024
FR = 128
FPART = FR // NS
VQ = 4
VW = VOX // VQ
OWN = 105

NN = (((1,), (0,)), ((), ()))
NT = (((1,), (1,)), ((), ()))
TN = (((0,), (0,)), ((), ()))


def dot(a, b, dims):
    return lax.dot_general(a, b, dims, preferred_element_type=F32)


def pieces(x):
    hi = x.astype(BF16)
    rest = x - hi.astype(F32)
    mid = rest.astype(BF16)
    low = (rest - mid.astype(F32)).astype(BF16)
    return hi, mid, low


def fan(values, oh_hi, oh_lo):
    parts = [jnp.where(oh_hi > 0, jnp.broadcast_to(p.astype(F32), oh_hi.shape), 0.0) for p in pieces(values)]
    lhs = jnp.concatenate(parts, axis=0).astype(BF16)
    out = dot(lhs, oh_lo, NT)
    return out[0:NV] + out[NV : 2 * NV] + out[2 * NV : 3 * NV]


CHUNKS = 4


def prepare(
    tile_bin, tile_vox, tile_count, subset, pairs, background, tiles,
    a_ref, pair_ref, back_ref,
    held, acc, half, in_sem, out_sem,
):
    size = held.shape[0] // CHUNKS

    def fetch(c):
        part = pl.ds(c * size, size)
        return pltpu.make_async_copy(tiles.at[part], held.at[part], in_sem.at[c])

    for c in range(CHUNKS):
        fetch(c).start()
    spots = []
    seen = [jnp.int32(0), jnp.int32(0)]
    for row in range(NB):
        k = subset[row]
        spots.append(jnp.where(k == 0, seen[0], NB // SUBSETS + seen[1]))
        seen = [seen[0] + jnp.where(k == 0, 1, 0), seen[1] + jnp.where(k == 0, 0, 1)]

    def spot_of(row):
        out = spots[0]
        for i in range(1, NB):
            out = jnp.where(row == i, spots[i], out)
        return out

    for row in range(NB):
        acc[row] = jnp.zeros((TB, VOX), F32)
        lanes = pl.ds(pl.multiple_of(spots[row] * TB, TB), TB)
        back_ref[:, lanes] = background[:, pl.ds(row * TB, TB)]
        pair_ref[:, lanes] = pairs[:, pl.ds(row * TB, TB)]

    for c in range(CHUNKS):
        fetch(c).wait()

        @pl.loop(c * size, jnp.minimum((c + 1) * size, tile_count[0, 0]))
        def _(t):
            p = spot_of(tile_bin[t])
            cols = pl.ds(pl.multiple_of(tile_vox[t] * TB, TB), TB)
            acc[p, :, cols] += held[t].astype(F32)

    def put(row):
        part = pl.ds(row * TB, TB)
        return pltpu.make_async_copy(half.at[part], a_ref.at[part], out_sem.at[row])

    for row in range(NB):
        half[pl.ds(row * TB, TB), :] = acc[row].astype(BF16)
        put(row).start()
    for row in range(NB):
        put(row).wait()


def finish(image_ref, gain_ref, out_ref, gain_out, held, in_sem, out_sem):
    size = VOX // CHUNKS

    def move(c, inward):
        part = pl.ds(c * size, size)
        if inward:
            return pltpu.make_async_copy(image_ref.at[part], held.at[part], in_sem.at[c])
        return pltpu.make_async_copy(held.at[part], out_ref.at[part], out_sem.at[c])

    for c in range(CHUNKS):
        move(c, True).start()
    gain_out[...] = gain_ref[...]
    for c in range(CHUNKS):
        move(c, True).wait()
        move(c, False).start()
    for c in range(CHUNKS):
        move(c, False).wait()


def exchange(
    subset, pair_ref, back_ref, efficiency, a_hbm, image_hbm, meas_hbm,
    out_hbm, gain_ref,
    a_ref, image, measured, img_t, meas_t, part_ref, eff_ref, out_ref,
    table, fwd_send, fwd, rat, sens_send, sens, bck_send, bck, img_send, img,
    sum_send, sums, fin, q_send, q_recv, fan_send, fan_recv,
    send_sem, recv_sem, copy_sem,
):
    v = lax.axis_index("view")
    s = lax.axis_index("slab")
    loads = [
        pltpu.make_async_copy(image_hbm, image, copy_sem.at[0]),
        pltpu.make_async_copy(a_hbm, a_ref, copy_sem.at[1]),
        pltpu.make_async_copy(meas_hbm, measured, copy_sem.at[2]),
    ]
    for load in loads:
        load.start()
    barrier = pltpu.get_barrier_semaphore()

    def view_peer(i):
        return lax.rem(v + i, NV)

    def slab_peer(i):
        return lax.rem(s + i, NS)

    @pl.loop(1, NV)
    def _(i):
        pl.semaphore_signal(barrier, inc=1, device_id=(view_peer(i), s), device_id_type=MESH)

    @pl.loop(1, NS)
    def _(i):
        pl.semaphore_signal(barrier, inc=1, device_id=(v, slab_peer(i)), device_id_type=MESH)

    loads[0].wait()
    for q in range(NB):
        img_t[:, pl.ds(q * TB, TB)] = image[q].T
    eff_ref[...] = jnp.zeros_like(eff_ref)
    eff_ref[0, :, 0:OWN] = efficiency[...]
    loads[1].wait()
    first = dot(img_t[...].astype(BF16), a_ref[0:HALF, :], NT)
    part_ref[...] = first.astype(BF16).reshape(NS, FPART, HALF)
    pl.semaphore_wait(barrier, NV - 1 + NS - 1)

    def to_views(phase, source, target):
        @pl.loop(1, NV)
        def _(i):
            w = view_peer(i)
            pltpu.make_async_remote_copy(
                src_ref=source(w), dst_ref=target, send_sem=send_sem.at[phase], recv_sem=recv_sem.at[phase],
                device_id=(w, s), device_id_type=MESH,
            ).start()

    def to_slabs(phase, source, target):
        @pl.loop(1, NS)
        def _(i):
            w = slab_peer(i)
            pltpu.make_async_remote_copy(
                src_ref=source(w), dst_ref=target, send_sem=send_sem.at[phase], recv_sem=recv_sem.at[phase],
                device_id=(v, w), device_id_type=MESH,
            ).start()

    def await_all(sem, ref):
        pltpu.make_async_copy(ref, ref, sem).wait()

    def views_of(ref):
        return ref.at[pl.ds(0, NV - 1)]

    def slabs_of(ref):
        return ref.at[pl.ds(0, NS - 1)]

    sent = [(0, slabs_of(fwd.at[0])), (1, views_of(table))]

    def part_of(w):
        return 2 * lax.rem(w // VQ, 4) + w // 16

    z = v // 16
    vi = lax.rem(v, VQ)
    fi = part_of(v)
    frames = pl.ds(pl.multiple_of(fi * FPART, FPART), FPART)
    slot = vi * NS + fi

    to_slabs(0, lambda w: part_ref.at[w], fwd.at[0, s])
    to_views(1, lambda w: eff_ref.at[0], table.at[v])
    fwd[0, s] = part_ref[s]
    table[v] = eff_ref[0]

    loads[2].wait()
    spots = []
    seen = [jnp.int32(0), jnp.int32(0)]
    for row in range(NB):
        k = subset[row]
        spots.append(jnp.where(k == 0, seen[0], NB // SUBSETS + seen[1]))
        seen = [seen[0] + jnp.where(k == 0, 1, 0), seen[1] + jnp.where(k == 0, 0, 1)]
    for p in range(NB):
        row = jnp.int32(0)
        for r in range(1, NB):
            row = jnp.where(spots[r] == p, r, row)
        meas_t[:, pl.ds(p * TB, TB)] = measured[row].T
    meas = meas_t[pl.ds(pl.multiple_of(s * FPART, FPART), FPART), :]
    est0 = img_t[frames, pl.ds(pl.multiple_of(vi * VW, VW), VW)]
    crystals = jnp.concatenate([pair_ref[0:1, :], pair_ref[1:2, :]], axis=1)
    high = jnp.floor((crystals.astype(F32) + 0.5) * (1.0 / OWN)).astype(jnp.int32)
    low = crystals - high * OWN
    oh_hi = jnp.where(lax.broadcasted_iota(jnp.int32, (NV, 2 * BINS), 0) == high, 1.0, 0.0)
    oh_lo = jnp.where(lax.broadcasted_iota(jnp.int32, (TB, 2 * BINS), 0) == low, 1.0, 0.0).astype(BF16)
    counted = jnp.sum(meas_t[...], axis=0, keepdims=True)
    counts = fan(jnp.concatenate([counted, counted], axis=1), oh_hi, oh_lo)
    fan_send[:, 0:1, :] = counts.reshape(NV, 1, TB)

    await_all(recv_sem.at[1], views_of(table))
    rows = table[...].reshape(NV, TB)
    cols = jnp.concatenate([p.astype(F32) for p in pieces(rows)], axis=0).astype(BF16)
    hi3 = jnp.concatenate([oh_hi, oh_hi, oh_hi], axis=0).astype(BF16)
    picked = dot(cols, hi3, TN)
    ends = jnp.sum(jnp.where(oh_lo > 0, picked, 0.0), axis=0, keepdims=True)
    weight = ends[:, 0:BINS] * ends[:, BINS : 2 * BINS]
    back = back_ref[...]

    phase = 2
    for k in range(SUBSETS):
        bins = slice(k * HALF, (k + 1) * HALF)
        w_k = weight[:, bins]
        fwd_phase = 0 if k == 0 else phase
        if k > 0:
            total = jnp.zeros((FR, HALF), F32)
            for q in range(VQ):
                quarter = img[q * NS : (q + 1) * NS].reshape(FR, VW)
                total = total + dot(quarter, a_ref[bins, q * VW : (q + 1) * VW], NT)
            fwd_send[...] = total.astype(BF16).reshape(NS, FPART, HALF)
            to_slabs(phase, lambda w: fwd_send.at[w], fwd.at[k, s])
            fwd[k, s] = fwd_send[s]
            sent.append((phase, slabs_of(fwd.at[k])))
            phase += 1
        await_all(recv_sem.at[fwd_phase], slabs_of(fwd.at[k]))
        summed = jnp.sum(fwd[k].astype(F32), axis=0)
        ratio = (w_k * meas[:, bins]) / (w_k * summed + back[:, bins])
        rat[k, s] = ratio.astype(BF16)
        to_slabs(phase, lambda w: rat.at[k, s], rat.at[k, s])
        rat_phase = phase
        sent.append((rat_phase, slabs_of(rat.at[k])))
        phase += 1

        if k == 0:
            row = lax.broadcasted_iota(jnp.int32, (16, BINS), 0)
            half = lax.broadcasted_iota(jnp.int32, (16, BINS), 1) // HALF
            lhs = jnp.where(row == half, jnp.broadcast_to(weight, (16, BINS)), 0.0).astype(BF16)
            both = dot(lhs, a_ref[...], NN)
            for q in range(VQ):
                sens_send[q] = both[0:SUBSETS, q * VW : (q + 1) * VW]
            sens_phase = phase
            phase += 1
            to_views(sens_phase, lambda w: sens_send.at[lax.rem(w, VQ)], sens.at[v])
            sens[v] = sens_send[vi]
            sent.append((sens_phase, views_of(sens)))

        await_all(recv_sem.at[rat_phase], slabs_of(rat.at[k]))
        lhs = rat[k].reshape(FR, HALF)
        for q in range(VQ):
            bck_send[k, q] = dot(lhs, a_ref[bins, q * VW : (q + 1) * VW], NN).astype(BF16)
        to_views(
            phase,
            lambda w: bck_send.at[k, lax.rem(w, VQ), pl.ds(pl.multiple_of(part_of(w) * FPART, FPART), FPART), :],
            bck.at[k, v],
        )
        bck[k, v] = bck_send[k, vi, frames, :]
        bck_phase = phase
        sent.append((bck_phase, views_of(bck.at[k])))
        phase += 1

        if k == 0:
            await_all(recv_sem.at[sens_phase], views_of(sens))
            sens_sum = jnp.sum(sens[...], axis=0)
            est = est0
        await_all(recv_sem.at[bck_phase], views_of(bck.at[k]))
        back_image = jnp.sum(bck[k].astype(F32), axis=0)
        est = est * (back_image + SMOOTH) / (sens_sum[k : k + 1, :] + SMOOTH)
        half_image = est.astype(BF16)
        if k < SUBSETS - 1:
            img_send[...] = half_image
            to_views(phase, lambda w: img_send, img.at[slot])
            img[slot] = half_image
            await_all(recv_sem.at[phase], views_of(img))
            sent.append((phase, views_of(img)))
            phase += 1

    part_sum = jnp.sum(half_image.astype(F32), axis=0, keepdims=True)
    sum_send[...] = part_sum
    sum_phase = phase
    to_views(sum_phase, lambda w: sum_send, sums.at[v])
    sums[v] = part_sum
    pair_phase, fin_phase = phase + 1, phase + 2
    phase += 3
    partner = lax.rem(v + 16, NV)
    fin[slot // 2, z] = est
    pair_copy = pltpu.make_async_remote_copy(
        src_ref=fin.at[slot // 2, z], dst_ref=fin.at[slot // 2, z],
        send_sem=send_sem.at[pair_phase], recv_sem=recv_sem.at[pair_phase],
        device_id=(partner, s), device_id_type=MESH,
    )
    pair_copy.start()
    await_all(recv_sem.at[sum_phase], views_of(sums))
    sent.append((sum_phase, views_of(sums)))
    pair_copy.wait_recv()

    @pl.loop(1, 16)
    def _(i):
        w = 16 * z + lax.rem(lax.rem(v, 16) + i, 16)
        pltpu.make_async_remote_copy(
            src_ref=fin.at[slot // 2], dst_ref=fin.at[slot // 2],
            send_sem=send_sem.at[fin_phase], recv_sem=recv_sem.at[fin_phase],
            device_id=(w, s), device_id_type=MESH,
        ).start()

    quarter = []
    for q in range(VQ):
        total = sums[q]
        for f in range(1, NS):
            total = total + sums[f * VQ + q]
        quarter.append(total)
    image_sum = jnp.concatenate(quarter, axis=1)
    row = lax.broadcasted_iota(jnp.int32, (16, VOX), 0)
    hi, mid, low = [jnp.broadcast_to(p.astype(F32), (16, VOX)) for p in pieces(image_sum)]
    lhs = jnp.where(row == 0, hi, jnp.where(row == 1, mid, jnp.where(row == 2, low, 0.0))).astype(BF16)
    bins_sum = jnp.sum(dot(lhs, a_ref[...], NT), axis=0, keepdims=True)
    q_send[...] = bins_sum
    to_slabs(phase, lambda w: q_send, q_recv.at[s])
    q_recv[s] = bins_sum
    await_all(recv_sem.at[phase], slabs_of(q_recv))
    sent.append((phase, slabs_of(q_recv)))
    phase += 1
    final = jnp.sum(q_recv[...], axis=0)
    expected = weight * final + FR * back
    fan_exp = fan(jnp.concatenate([expected, expected], axis=1), oh_hi, oh_lo)
    fan_send[:, 1:2, :] = fan_exp.reshape(NV, 1, TB)
    to_views(phase, lambda w: fan_send.at[w], fan_recv.at[v])
    fan_recv[v] = fan_send[v]

    others = fin.at[pl.ds(0, 15)]
    await_all(recv_sem.at[fin_phase], others)
    for q in range(VQ):
        part = pl.ds(q * VW, VW)
        out_ref[part, :] = fin[q * 4 : (q + 1) * 4].reshape(FR, VW).T
        pltpu.make_async_copy(out_ref.at[part], out_hbm.at[part], copy_sem.at[3 + q]).start()

    await_all(recv_sem.at[phase], views_of(fan_recv))
    totals = jnp.sum(fan_recv[...], axis=0)
    gain = eff_ref[0] * (totals[0:1, :] + FAN_OFFSET) / (totals[1:2, :] + FAN_OFFSET)
    gain_ref[...] = gain[:, 0:OWN]
    sent.append((phase, views_of(fan_recv)))
    sent.append((fin_phase, others))
    for number, ref in sent:
        await_all(send_sem.at[number], ref)
    pair_copy.wait_send()
    for q in range(VQ):
        part = pl.ds(q * VW, VW)
        pltpu.make_async_copy(out_ref.at[part], out_hbm.at[part], copy_sem.at[3 + q]).wait()


PHASES = 14


def on_device(
    tiles, tile_bin, tile_vox, tile_count, subset, pairs, measured, background, image, efficiency
):
    smem = pl.BlockSpec(memory_space=SMEM)
    vmem = pl.BlockSpec(memory_space=VMEM)
    hbm = pl.BlockSpec(memory_space=pl.ANY)
    shape = jax.ShapeDtypeStruct
    dma = pltpu.SemaphoreType.DMA
    count = tiles.shape[2]
    projector, ends, back = pl.pallas_call(
        prepare,
        out_shape=(shape((BINS, VOX), BF16), shape((2, BINS), jnp.int32), shape((1, BINS), F32)),
        in_specs=[smem] * 4 + [vmem, vmem, hbm],
        out_specs=(hbm, vmem, vmem),
        scratch_shapes=[
            VMEM((count, TB, TB), BF16),
            VMEM((NB, TB, VOX), F32),
            VMEM((BINS, VOX), BF16),
            dma((CHUNKS,)),
            dma((NB,)),
        ],
        name="prepare",
    )(
        tile_bin.reshape(-1),
        tile_vox.reshape(-1),
        tile_count,
        subset,
        pairs,
        background.reshape(1, BINS),
        tiles.reshape(tiles.shape[2:]),
    )
    image_out, gain = pl.pallas_call(
        exchange,
        out_shape=(shape((VOX, FR), F32), shape((1, OWN), F32)),
        in_specs=[smem, vmem, vmem, vmem, hbm, hbm, hbm],
        out_specs=(hbm, vmem),
        scratch_shapes=[
            VMEM((BINS, VOX), BF16),
            VMEM((NB, TB, FR), F32),
            VMEM((NB, TB, FR), F32),
            VMEM((FR, VOX), F32),
            VMEM((FR, BINS), F32),
            VMEM((NS, FPART, HALF), BF16),
            VMEM((1, 1, TB), F32),
            VMEM((VOX, FR), F32),
            VMEM((NV, 1, TB), F32),
            VMEM((NS, FPART, HALF), BF16),
            VMEM((SUBSETS, NS, FPART, HALF), BF16),
            VMEM((SUBSETS, NS, FPART, HALF), BF16),
            VMEM((VQ, SUBSETS, VW), F32),
            VMEM((NV, SUBSETS, VW), F32),
            VMEM((SUBSETS, VQ, FR, VW), BF16),
            VMEM((SUBSETS, NV, FPART, VW), BF16),
            VMEM((FPART, VW), BF16),
            VMEM((NV, FPART, VW), BF16),
            VMEM((1, VW), F32),
            VMEM((NV, 1, VW), F32),
            VMEM((NV // 2, 2, FPART, VW), F32),
            VMEM((1, BINS), F32),
            VMEM((NS, 1, BINS), F32),
            VMEM((NV, 2, TB), F32),
            VMEM((NV, 2, TB), F32),
            dma((PHASES,)),
            dma((PHASES,)),
            dma((3 + VQ,)),
        ],
        compiler_params=pltpu.CompilerParams(collective_id=0, has_side_effects=True),
        name="exchange",
    )(
        subset,
        ends,
        back,
        efficiency.reshape(1, OWN),
        projector,
        image.reshape(NB, TB, FR),
        measured.reshape(NB, TB, FR),
    )
    image_out, gain = pl.pallas_call(
        finish,
        out_shape=(shape((VOX, FR), F32), shape((1, OWN), F32)),
        in_specs=[hbm, vmem],
        out_specs=(hbm, vmem),
        scratch_shapes=[VMEM((VOX, FR), F32), dma((CHUNKS,)), dma((CHUNKS,))],
        name="finish",
    )(image_out, gain)
    return image_out, gain.reshape(OWN)


def solution(mesh):
    return jax.shard_map(
        on_device,
        mesh=mesh,
        in_specs=(
            P("view", "slab", None, None, None),
            P("view", "slab", None),
            P("view", "slab", None),
            P("view", "slab"),
            P("view"),
            P(None, "view"),
            P("view", None),
            P("view"),
            P("slab", None),
            P("view"),
        ),
        out_specs=(P("slab", None), P("view")),
        check_vma=False,
    )
```

```python
import jax
import jax.numpy as jnp
from jax import lax
from jax.experimental import pallas as pl
from jax.experimental.pallas import tpu as pltpu
from jax.sharding import PartitionSpec as P

SUBSETS = 2
SMOOTH = 0.1
FAN_OFFSET = 1.0
MESH = pl.DeviceIdType.MESH
F32 = jnp.float32
BF16 = jnp.bfloat16
VMEM = pltpu.VMEM
SMEM = pltpu.SMEM

NV = 32
NS = 8
TB = 128
NB = 8
BINS = 1024
HALF = BINS // SUBSETS
VOX = 1024
FR = 128
FPART = FR // NS
VQ = 4
VW = VOX // VQ
OWN = 105

NN = (((1,), (0,)), ((), ()))
NT = (((1,), (1,)), ((), ()))
TN = (((0,), (0,)), ((), ()))


def dot(a, b, dims):
    return lax.dot_general(a, b, dims, preferred_element_type=F32)


def pieces(x):
    hi = x.astype(BF16)
    rest = x - hi.astype(F32)
    mid = rest.astype(BF16)
    low = (rest - mid.astype(F32)).astype(BF16)
    return hi, mid, low


def fan(values, oh_hi, oh_lo):
    parts = [jnp.where(oh_hi > 0, jnp.broadcast_to(p.astype(F32), oh_hi.shape), 0.0) for p in pieces(values)]
    lhs = jnp.concatenate(parts, axis=0).astype(BF16)
    out = dot(lhs, oh_lo, NT)
    return out[0:NV] + out[NV : 2 * NV] + out[2 * NV : 3 * NV]


def exchange(
    tile_count, subset, tile_bin, tile_vox, pairs, background, efficiency, tiles_hbm, image_hbm, meas_hbm,
    out_ref, gain_ref,
    a_ref, tiles, runs, keys, plan, plan_s, back_ref, pair_ref, image, measured, img_t, meas_t, part_ref, eff_ref,
    table, fwd_send, fwd, rat, sens_send, sens, bck_send, bck, img_send, img,
    sum_send, sums, fin, q_send, q_recv, fan_send, fan_recv,
    send_sem, recv_sem, copy_sem,
):
    v = lax.axis_index("view")
    s = lax.axis_index("slab")
    loads = [
        pltpu.make_async_copy(image_hbm, image, copy_sem.at[0]),
        pltpu.make_async_copy(tiles_hbm, tiles, copy_sem.at[1]),
        pltpu.make_async_copy(meas_hbm, measured, copy_sem.at[2]),
    ]
    for load in loads:
        load.start()
    barrier = pltpu.get_barrier_semaphore()

    def view_peer(i):
        return lax.rem(v + i, NV)

    def slab_peer(i):
        return lax.rem(s + i, NS)

    @pl.loop(1, NV)
    def _(i):
        pl.semaphore_signal(barrier, inc=1, device_id=(view_peer(i), s), device_id_type=MESH)

    @pl.loop(1, NS)
    def _(i):
        pl.semaphore_signal(barrier, inc=1, device_id=(v, slab_peer(i)), device_id_type=MESH)

    spots = []
    seen = [jnp.int32(0), jnp.int32(0)]
    for row in range(NB):
        k = subset[row]
        spots.append(jnp.where(k == 0, seen[0], NB // SUBSETS + seen[1]))
        seen = [seen[0] + jnp.where(k == 0, 1, 0), seen[1] + jnp.where(k == 0, 0, 1)]
    rows_at = []
    for p in range(NB):
        row = jnp.int32(0)
        for r in range(1, NB):
            row = jnp.where(spots[r] == p, r, row)
        rows_at.append(row)

    count = tiles.shape[0]
    where_bin = tile_bin[...]
    key = jnp.zeros_like(where_bin)
    for r in range(NB):
        key = jnp.where(where_bin == r, spots[r], key)
    key = key * NB + tile_vox[...]
    live = lax.broadcasted_iota(jnp.int32, key.shape, 1) < tile_count[0, 0]
    keys[...] = jnp.full_like(keys, NB * NB)
    keys[:, 0:count] = jnp.where(live, key, NB * NB)
    sub = lax.broadcasted_iota(jnp.int32, (TB, TB), 0)
    lane = lax.broadcasted_iota(jnp.int32, (TB, TB), 1)
    across = jnp.broadcast_to(keys[...], (TB, TB))
    down = across.T
    before = (down < across) | ((down == across) & (sub < lane))
    rank = jnp.sum(jnp.where(before, 1, 0), axis=0, keepdims=True)
    chosen = jnp.broadcast_to(rank, (TB, TB)).T == lane
    plan[...] = jnp.zeros_like(plan)
    plan[0:1, :] = jnp.sum(jnp.where(chosen, sub, 0), axis=0, keepdims=True)
    plan[1:2, :] = jnp.sum(jnp.where(chosen, down, 0), axis=0, keepdims=True)
    plan[2:3, :] = jnp.sum(jnp.where(down <= lane, 1, 0), axis=0, keepdims=True)
    to_scalars = pltpu.make_async_copy(plan, plan_s, copy_sem.at[3])
    to_scalars.start()
    loads[0].wait()
    for q in range(NB):
        img_t[:, pl.ds(q * TB, TB)] = image[q].T
    eff_ref[...] = jnp.zeros_like(eff_ref)
    eff_ref[0, :, 0:OWN] = efficiency[...]
    to_scalars.wait()
    loads[1].wait()

    def add_tile(r, total):
        same = plan_s[1, r] == plan_s[1, jnp.maximum(r - 1, 0)]
        total = total * jnp.where(same, 1.0, 0.0) + tiles[plan_s[0, r]].astype(F32)
        runs[r] = total
        return total

    lax.fori_loop(0, count, add_tile, jnp.zeros((TB, TB), F32), unroll=2)

    @pl.loop(0, NB * NB, unroll=2)
    def _(d):
        ends_at = plan_s[2, d]
        starts_at = jnp.where(d == 0, 0, plan_s[2, jnp.maximum(d - 1, 0)])
        kept = jnp.where(ends_at > starts_at, 1.0, 0.0)
        block = runs[jnp.maximum(ends_at - 1, 0)] * kept
        part = pl.ds(pl.multiple_of((d // NB) * TB, TB), TB)
        a_ref[part, pl.ds(pl.multiple_of((d % NB) * TB, TB), TB)] = block.astype(BF16)

    first = dot(img_t[...].astype(BF16), a_ref[0:HALF, :], NT)
    part_ref[...] = first.astype(BF16).reshape(NS, FPART, HALF)
    pl.semaphore_wait(barrier, NV - 1 + NS - 1)

    def to_views(phase, source, target):
        @pl.loop(1, NV)
        def _(i):
            w = view_peer(i)
            pltpu.make_async_remote_copy(
                src_ref=source(w), dst_ref=target, send_sem=send_sem.at[phase], recv_sem=recv_sem.at[phase],
                device_id=(w, s), device_id_type=MESH,
            ).start()

    def to_slabs(phase, source, target):
        @pl.loop(1, NS)
        def _(i):
            w = slab_peer(i)
            pltpu.make_async_remote_copy(
                src_ref=source(w), dst_ref=target, send_sem=send_sem.at[phase], recv_sem=recv_sem.at[phase],
                device_id=(v, w), device_id_type=MESH,
            ).start()

    def await_all(sem, ref):
        pltpu.make_async_copy(ref, ref, sem).wait()

    def views_of(ref):
        return ref.at[pl.ds(0, NV - 1)]

    def slabs_of(ref):
        return ref.at[pl.ds(0, NS - 1)]

    sent = [(0, slabs_of(fwd.at[0])), (1, views_of(table))]

    def part_of(w):
        return 2 * lax.rem(w // VQ, 4) + w // 16

    z = v // 16
    vi = lax.rem(v, VQ)
    fi = part_of(v)
    frames = pl.ds(pl.multiple_of(fi * FPART, FPART), FPART)
    slot = vi * NS + fi

    to_slabs(0, lambda w: part_ref.at[w], fwd.at[0, s])
    to_views(1, lambda w: eff_ref.at[0], table.at[v])
    fwd[0, s] = part_ref[s]
    table[v] = eff_ref[0]

    loads[2].wait()
    for p in range(NB):
        part = pl.ds(p * TB, TB)
        meas_t[:, part] = measured[rows_at[p]].T
        noise = background[:, 0:TB]
        pair = pairs[:, 0:TB]
        for r in range(1, NB):
            noise = jnp.where(spots[r] == p, background[:, r * TB : (r + 1) * TB], noise)
            pair = jnp.where(spots[r] == p, pairs[:, r * TB : (r + 1) * TB], pair)
        back_ref[:, part] = noise
        pair_ref[:, part] = pair
    meas = meas_t[pl.ds(pl.multiple_of(s * FPART, FPART), FPART), :]
    est0 = img_t[frames, pl.ds(pl.multiple_of(vi * VW, VW), VW)]
    crystals = jnp.concatenate([pair_ref[0:1, :], pair_ref[1:2, :]], axis=1)
    high = jnp.floor((crystals.astype(F32) + 0.5) * (1.0 / OWN)).astype(jnp.int32)
    low = crystals - high * OWN
    oh_hi = jnp.where(lax.broadcasted_iota(jnp.int32, (NV, 2 * BINS), 0) == high, 1.0, 0.0)
    oh_lo = jnp.where(lax.broadcasted_iota(jnp.int32, (TB, 2 * BINS), 0) == low, 1.0, 0.0).astype(BF16)
    counted = jnp.sum(meas_t[...], axis=0, keepdims=True)
    counts = fan(jnp.concatenate([counted, counted], axis=1), oh_hi, oh_lo)
    fan_send[:, 0:1, :] = counts.reshape(NV, 1, TB)

    await_all(recv_sem.at[1], views_of(table))
    rows = table[...].reshape(NV, TB)
    cols = jnp.concatenate([p.astype(F32) for p in pieces(rows)], axis=0).astype(BF16)
    hi3 = jnp.concatenate([oh_hi, oh_hi, oh_hi], axis=0).astype(BF16)
    picked = dot(cols, hi3, TN)
    ends = jnp.sum(jnp.where(oh_lo > 0, picked, 0.0), axis=0, keepdims=True)
    weight = ends[:, 0:BINS] * ends[:, BINS : 2 * BINS]
    back = back_ref[...]

    phase = 2
    for k in range(SUBSETS):
        bins = slice(k * HALF, (k + 1) * HALF)
        w_k = weight[:, bins]
        fwd_phase = 0 if k == 0 else phase
        if k > 0:
            total = jnp.zeros((FR, HALF), F32)
            for q in range(VQ):
                quarter = img[q * NS : (q + 1) * NS].reshape(FR, VW)
                total = total + dot(quarter, a_ref[bins, q * VW : (q + 1) * VW], NT)
            fwd_send[...] = total.astype(BF16).reshape(NS, FPART, HALF)
            to_slabs(phase, lambda w: fwd_send.at[w], fwd.at[k, s])
            fwd[k, s] = fwd_send[s]
            sent.append((phase, slabs_of(fwd.at[k])))
            phase += 1
        await_all(recv_sem.at[fwd_phase], slabs_of(fwd.at[k]))
        summed = jnp.sum(fwd[k].astype(F32), axis=0)
        ratio = (w_k * meas[:, bins]) / (w_k * summed + back[:, bins])
        rat[k, s] = ratio.astype(BF16)
        to_slabs(phase, lambda w: rat.at[k, s], rat.at[k, s])
        rat_phase = phase
        sent.append((rat_phase, slabs_of(rat.at[k])))
        phase += 1

        if k == 0:
            row = lax.broadcasted_iota(jnp.int32, (16, BINS), 0)
            half = lax.broadcasted_iota(jnp.int32, (16, BINS), 1) // HALF
            lhs = jnp.where(row == half, jnp.broadcast_to(weight, (16, BINS)), 0.0).astype(BF16)
            both = dot(lhs, a_ref[...], NN)
            for q in range(VQ):
                sens_send[q] = both[0:SUBSETS, q * VW : (q + 1) * VW]
            sens_phase = phase
            phase += 1
            to_views(sens_phase, lambda w: sens_send.at[lax.rem(w, VQ)], sens.at[v])
            sens[v] = sens_send[vi]
            sent.append((sens_phase, views_of(sens)))

        await_all(recv_sem.at[rat_phase], slabs_of(rat.at[k]))
        lhs = rat[k].reshape(FR, HALF)
        for q in range(VQ):
            bck_send[k, q] = dot(lhs, a_ref[bins, q * VW : (q + 1) * VW], NN).astype(BF16)
        to_views(
            phase,
            lambda w: bck_send.at[k, lax.rem(w, VQ), pl.ds(pl.multiple_of(part_of(w) * FPART, FPART), FPART), :],
            bck.at[k, v],
        )
        bck[k, v] = bck_send[k, vi, frames, :]
        bck_phase = phase
        sent.append((bck_phase, views_of(bck.at[k])))
        phase += 1

        if k == 0:
            await_all(recv_sem.at[sens_phase], views_of(sens))
            sens_sum = jnp.sum(sens[...], axis=0)
            est = est0
        await_all(recv_sem.at[bck_phase], views_of(bck.at[k]))
        back_image = jnp.sum(bck[k].astype(F32), axis=0)
        est = est * (back_image + SMOOTH) / (sens_sum[k : k + 1, :] + SMOOTH)
        half_image = est.astype(BF16)
        if k < SUBSETS - 1:
            img_send[...] = half_image
            to_views(phase, lambda w: img_send, img.at[slot])
            img[slot] = half_image
            await_all(recv_sem.at[phase], views_of(img))
            sent.append((phase, views_of(img)))
            phase += 1

    part_sum = jnp.sum(half_image.astype(F32), axis=0, keepdims=True)
    sum_send[...] = part_sum
    sum_phase = phase
    to_views(sum_phase, lambda w: sum_send, sums.at[v])
    sums[v] = part_sum
    pair_phase, fin_phase = phase + 1, phase + 2
    phase += 3
    partner = lax.rem(v + 16, NV)
    fin[slot // 2, z] = est
    pair_copy = pltpu.make_async_remote_copy(
        src_ref=fin.at[slot // 2, z], dst_ref=fin.at[slot // 2, z],
        send_sem=send_sem.at[pair_phase], recv_sem=recv_sem.at[pair_phase],
        device_id=(partner, s), device_id_type=MESH,
    )
    pair_copy.start()
    await_all(recv_sem.at[sum_phase], views_of(sums))
    sent.append((sum_phase, views_of(sums)))
    pair_copy.wait_recv()

    @pl.loop(1, 16)
    def _(i):
        w = 16 * z + lax.rem(lax.rem(v, 16) + i, 16)
        pltpu.make_async_remote_copy(
            src_ref=fin.at[slot // 2], dst_ref=fin.at[slot // 2],
            send_sem=send_sem.at[fin_phase], recv_sem=recv_sem.at[fin_phase],
            device_id=(w, s), device_id_type=MESH,
        ).start()

    quarter = []
    for q in range(VQ):
        total = sums[q]
        for f in range(1, NS):
            total = total + sums[f * VQ + q]
        quarter.append(total)
    image_sum = jnp.concatenate(quarter, axis=1)
    row = lax.broadcasted_iota(jnp.int32, (16, VOX), 0)
    hi, mid, low = [jnp.broadcast_to(p.astype(F32), (16, VOX)) for p in pieces(image_sum)]
    lhs = jnp.where(row == 0, hi, jnp.where(row == 1, mid, jnp.where(row == 2, low, 0.0))).astype(BF16)
    bins_sum = jnp.sum(dot(lhs, a_ref[...], NT), axis=0, keepdims=True)
    q_send[...] = bins_sum
    to_slabs(phase, lambda w: q_send, q_recv.at[s])
    q_recv[s] = bins_sum
    await_all(recv_sem.at[phase], slabs_of(q_recv))
    sent.append((phase, slabs_of(q_recv)))
    phase += 1
    final = jnp.sum(q_recv[...], axis=0)
    expected = weight * final + FR * back
    fan_exp = fan(jnp.concatenate([expected, expected], axis=1), oh_hi, oh_lo)
    fan_send[:, 1:2, :] = fan_exp.reshape(NV, 1, TB)
    to_views(phase, lambda w: fan_send.at[w], fan_recv.at[v])
    fan_recv[v] = fan_send[v]

    others = fin.at[pl.ds(0, 15)]
    await_all(recv_sem.at[fin_phase], others)
    for q in range(VQ):
        part = pl.ds(q * VW, VW)
        out_ref[part, :] = fin[q * 4 : (q + 1) * 4].reshape(FR, VW).T

    await_all(recv_sem.at[phase], views_of(fan_recv))
    totals = jnp.sum(fan_recv[...], axis=0)
    gain = eff_ref[0] * (totals[0:1, :] + FAN_OFFSET) / (totals[1:2, :] + FAN_OFFSET)
    gain_ref[...] = gain[:, 0:OWN]
    sent.append((phase, views_of(fan_recv)))
    sent.append((fin_phase, others))
    for number, ref in sent:
        await_all(send_sem.at[number], ref)
    pair_copy.wait_send()


PHASES = 14


def on_device(
    tiles, tile_bin, tile_vox, tile_count, subset, pairs, measured, background, image, efficiency
):
    smem = pl.BlockSpec(memory_space=SMEM)
    vmem = pl.BlockSpec(memory_space=VMEM)
    hbm = pl.BlockSpec(memory_space=pl.ANY)
    shape = jax.ShapeDtypeStruct
    dma = pltpu.SemaphoreType.DMA
    count = tiles.shape[2]
    image_out, gain = pl.pallas_call(
        exchange,
        out_shape=(VMEM((VOX, FR), F32), VMEM((1, OWN), F32)),
        in_specs=[smem, smem] + [vmem] * 5 + [hbm] * 3,
        out_specs=(vmem, vmem),
        scratch_shapes=[
            VMEM((BINS, VOX), BF16),
            VMEM((count, TB, TB), BF16),
            VMEM((count, TB, TB), F32),
            VMEM((1, TB), jnp.int32),
            VMEM((8, TB), jnp.int32),
            SMEM((8, TB), jnp.int32),
            VMEM((1, BINS), F32),
            VMEM((2, BINS), jnp.int32),
            VMEM((NB, TB, FR), F32),
            VMEM((NB, TB, FR), F32),
            VMEM((FR, VOX), F32),
            VMEM((FR, BINS), F32),
            VMEM((NS, FPART, HALF), BF16),
            VMEM((1, 1, TB), F32),
            VMEM((NV, 1, TB), F32),
            VMEM((NS, FPART, HALF), BF16),
            VMEM((SUBSETS, NS, FPART, HALF), BF16),
            VMEM((SUBSETS, NS, FPART, HALF), BF16),
            VMEM((VQ, SUBSETS, VW), F32),
            VMEM((NV, SUBSETS, VW), F32),
            VMEM((SUBSETS, VQ, FR, VW), BF16),
            VMEM((SUBSETS, NV, FPART, VW), BF16),
            VMEM((FPART, VW), BF16),
            VMEM((NV, FPART, VW), BF16),
            VMEM((1, VW), F32),
            VMEM((NV, 1, VW), F32),
            VMEM((NV // 2, 2, FPART, VW), F32),
            VMEM((1, BINS), F32),
            VMEM((NS, 1, BINS), F32),
            VMEM((NV, 2, TB), F32),
            VMEM((NV, 2, TB), F32),
            dma((PHASES,)),
            dma((PHASES,)),
            dma((4,)),
        ],
        compiler_params=pltpu.CompilerParams(collective_id=0, has_side_effects=True),
        name="exchange",
    )(
        tile_count,
        subset,
        tile_bin.reshape(1, count),
        tile_vox.reshape(1, count),
        pairs,
        background.reshape(1, BINS),
        efficiency.reshape(1, OWN),
        tiles.reshape(tiles.shape[2:]),
        image.reshape(NB, TB, FR),
        measured.reshape(NB, TB, FR),
    )
    return image_out, gain.reshape(OWN)


def solution(mesh):
    return jax.shard_map(
        on_device,
        mesh=mesh,
        in_specs=(
            P("view", "slab", None, None, None),
            P("view", "slab", None),
            P("view", "slab", None),
            P("view", "slab"),
            P("view"),
            P(None, "view"),
            P("view", None),
            P("view"),
            P("slab", None),
            P("view"),
        ),
        out_specs=(P("slab", None), P("view")),
        check_vma=False,
    )
```

```python
import jax
import jax.numpy as jnp
from jax import lax
from jax.experimental import pallas as pl
from jax.experimental.pallas import tpu as pltpu
from jax.sharding import PartitionSpec as P

SUBSETS = 2
SMOOTH = 0.1
FAN_OFFSET = 1.0
MESH = pl.DeviceIdType.MESH
F32 = jnp.float32
BF16 = jnp.bfloat16
VMEM = pltpu.VMEM
SMEM = pltpu.SMEM

NV = 32
NS = 8
TB = 128
NB = 8
BINS = 1024
HALF = BINS // SUBSETS
VOX = 1024
FR = 128
STREAMS = 2
FS = FR // STREAMS
FPART = FS // NS
VQ = 4
VW = VOX // VQ
OWN = 105

NN = (((1,), (0,)), ((), ()))
NT = (((1,), (1,)), ((), ()))
TN = (((0,), (0,)), ((), ()))


def dot(a, b, dims):
    return lax.dot_general(a, b, dims, preferred_element_type=F32)


def pieces(x):
    hi = x.astype(BF16)
    rest = x - hi.astype(F32)
    mid = rest.astype(BF16)
    low = (rest - mid.astype(F32)).astype(BF16)
    return hi, mid, low


def fan(values, oh_hi, oh_lo):
    parts = [jnp.where(oh_hi > 0, jnp.broadcast_to(p.astype(F32), oh_hi.shape), 0.0) for p in pieces(values)]
    lhs = jnp.concatenate(parts, axis=0).astype(BF16)
    out = dot(lhs, oh_lo, NT)
    return out[0:NV] + out[NV : 2 * NV] + out[2 * NV : 3 * NV]


def exchange(
    tile_count, subset, tile_bin, tile_vox, pairs, background, efficiency, tiles_hbm, image_hbm, meas_hbm,
    out_ref, gain_ref,
    a_ref, tiles, runs, keys, plan, plan_s, back_ref, pair_ref, image, measured, img_t, meas_t, part_ref, eff_ref,
    table, fwd_send, fwd, rat, sens_send, sens, bck_send, bck, img_send, img,
    sum_send, sums, fin, q_send, q_recv, fan_send, fan_recv,
    send_sem, recv_sem, copy_sem,
):
    v = lax.axis_index("view")
    s = lax.axis_index("slab")
    loads = [
        pltpu.make_async_copy(image_hbm, image, copy_sem.at[0]),
        pltpu.make_async_copy(tiles_hbm, tiles, copy_sem.at[1]),
        pltpu.make_async_copy(meas_hbm, measured, copy_sem.at[2]),
    ]
    for load in loads:
        load.start()
    barrier = pltpu.get_barrier_semaphore()

    def view_peer(i):
        return lax.rem(v + i, NV)

    def slab_peer(i):
        return lax.rem(s + i, NS)

    @pl.loop(1, NV)
    def _(i):
        pl.semaphore_signal(barrier, inc=1, device_id=(view_peer(i), s), device_id_type=MESH)

    @pl.loop(1, NS)
    def _(i):
        pl.semaphore_signal(barrier, inc=1, device_id=(v, slab_peer(i)), device_id_type=MESH)

    spots = []
    seen = [jnp.int32(0), jnp.int32(0)]
    for row in range(NB):
        k = subset[row]
        spots.append(jnp.where(k == 0, seen[0], NB // SUBSETS + seen[1]))
        seen = [seen[0] + jnp.where(k == 0, 1, 0), seen[1] + jnp.where(k == 0, 0, 1)]
    rows_at = []
    for p in range(NB):
        row = jnp.int32(0)
        for r in range(1, NB):
            row = jnp.where(spots[r] == p, r, row)
        rows_at.append(row)

    count = tiles.shape[0]
    where_bin = tile_bin[...]
    key = jnp.zeros_like(where_bin)
    for r in range(NB):
        key = jnp.where(where_bin == r, spots[r], key)
    key = key * NB + tile_vox[...]
    live = lax.broadcasted_iota(jnp.int32, key.shape, 1) < tile_count[0, 0]
    keys[...] = jnp.full_like(keys, NB * NB)
    keys[:, 0:count] = jnp.where(live, key, NB * NB)
    sub = lax.broadcasted_iota(jnp.int32, (TB, TB), 0)
    lane = lax.broadcasted_iota(jnp.int32, (TB, TB), 1)
    across = jnp.broadcast_to(keys[...], (TB, TB))
    down = across.T
    before = (down < across) | ((down == across) & (sub < lane))
    rank = jnp.sum(jnp.where(before, 1, 0), axis=0, keepdims=True)
    chosen = jnp.broadcast_to(rank, (TB, TB)).T == lane
    plan[...] = jnp.zeros_like(plan)
    plan[0:1, :] = jnp.sum(jnp.where(chosen, sub, 0), axis=0, keepdims=True)
    plan[1:2, :] = jnp.sum(jnp.where(chosen, down, 0), axis=0, keepdims=True)
    plan[2:3, :] = jnp.sum(jnp.where(down <= lane, 1, 0), axis=0, keepdims=True)
    to_scalars = pltpu.make_async_copy(plan, plan_s, copy_sem.at[3])
    to_scalars.start()
    loads[0].wait()
    for q in range(NB):
        img_t[:, pl.ds(q * TB, TB)] = image[q].T
    eff_ref[...] = jnp.zeros_like(eff_ref)
    eff_ref[0, :, 0:OWN] = efficiency[...]
    to_scalars.wait()
    loads[1].wait()

    def add_tile(r, total):
        same = plan_s[1, r] == plan_s[1, jnp.maximum(r - 1, 0)]
        total = total * jnp.where(same, 1.0, 0.0) + tiles[plan_s[0, r]].astype(F32)
        runs[r] = total
        return total

    lax.fori_loop(0, count, add_tile, jnp.zeros((TB, TB), F32), unroll=2)

    @pl.loop(0, NB * NB, unroll=2)
    def _(d):
        ends_at = plan_s[2, d]
        starts_at = jnp.where(d == 0, 0, plan_s[2, jnp.maximum(d - 1, 0)])
        kept = jnp.where(ends_at > starts_at, 1.0, 0.0)
        block = runs[jnp.maximum(ends_at - 1, 0)] * kept
        part = pl.ds(pl.multiple_of((d // NB) * TB, TB), TB)
        a_ref[part, pl.ds(pl.multiple_of((d % NB) * TB, TB), TB)] = block.astype(BF16)

    first = dot(img_t[...].astype(BF16), a_ref[0:HALF, :], NT)
    part_ref[...] = first.reshape(STREAMS, NS, FPART, HALF).astype(BF16)
    pl.semaphore_wait(barrier, NV - 1 + NS - 1)

    def to_views(phase, source, target):
        @pl.loop(1, NV)
        def _(i):
            w = view_peer(i)
            pltpu.make_async_remote_copy(
                src_ref=source(w), dst_ref=target, send_sem=send_sem.at[phase], recv_sem=recv_sem.at[phase],
                device_id=(w, s), device_id_type=MESH,
            ).start()

    def to_slabs(phase, source, target):
        @pl.loop(1, NS)
        def _(i):
            w = slab_peer(i)
            pltpu.make_async_remote_copy(
                src_ref=source(w), dst_ref=target, send_sem=send_sem.at[phase], recv_sem=recv_sem.at[phase],
                device_id=(v, w), device_id_type=MESH,
            ).start()

    def await_all(sem, ref):
        pltpu.make_async_copy(ref, ref, sem).wait()

    def views_of(ref):
        return ref.at[pl.ds(0, NV - 1)]

    def slabs_of(ref):
        return ref.at[pl.ds(0, NS - 1)]

    sent = []
    numbers = iter(range(PHASES))

    def new_phase(ref):
        number = next(numbers)
        sent.append((number, ref))
        return number

    def await_phase(number):
        await_all(recv_sem.at[number], dict(sent)[number])


    def part_of(w):
        return 2 * lax.rem(w // VQ, 4) + w // 16

    z = v // 16
    vi = lax.rem(v, VQ)
    fi = part_of(v)
    slot = vi * NS + fi

    fwd_at = [new_phase(slabs_of(fwd.at[0, h])) for h in range(STREAMS)]
    eff_at = new_phase(views_of(table))
    to_slabs(fwd_at[0], lambda w: part_ref.at[0, w], fwd.at[0, 0, s])
    to_views(eff_at, lambda w: eff_ref.at[0], table.at[v])
    for h in range(1, STREAMS):
        to_slabs(fwd_at[h], lambda w: part_ref.at[h, w], fwd.at[0, h, s])
    for h in range(STREAMS):
        fwd[0, h, s] = part_ref[h, s]
    table[v] = eff_ref[0]

    loads[2].wait()
    for p in range(NB):
        part = pl.ds(p * TB, TB)
        meas_t[:, part] = measured[rows_at[p]].T
        noise = background[:, 0:TB]
        pair = pairs[:, 0:TB]
        for r in range(1, NB):
            noise = jnp.where(spots[r] == p, background[:, r * TB : (r + 1) * TB], noise)
            pair = jnp.where(spots[r] == p, pairs[:, r * TB : (r + 1) * TB], pair)
        back_ref[:, part] = noise
        pair_ref[:, part] = pair
    meas = [meas_t[pl.ds(pl.multiple_of(h * FS + s * FPART, FPART), FPART), :] for h in range(STREAMS)]
    own = pl.ds(pl.multiple_of(vi * VW, VW), VW)
    est = [img_t[pl.ds(pl.multiple_of(h * FS + fi * FPART, FPART), FPART), own] for h in range(STREAMS)]
    crystals = jnp.concatenate([pair_ref[0:1, :], pair_ref[1:2, :]], axis=1)
    high = jnp.floor((crystals.astype(F32) + 0.5) * (1.0 / OWN)).astype(jnp.int32)
    low = crystals - high * OWN
    oh_hi = jnp.where(lax.broadcasted_iota(jnp.int32, (NV, 2 * BINS), 0) == high, 1.0, 0.0)
    oh_lo = jnp.where(lax.broadcasted_iota(jnp.int32, (TB, 2 * BINS), 0) == low, 1.0, 0.0).astype(BF16)
    counted = jnp.sum(meas_t[...], axis=0, keepdims=True)
    counts = fan(jnp.concatenate([counted, counted], axis=1), oh_hi, oh_lo)
    fan_send[:, 0:1, :] = counts.reshape(NV, 1, TB)

    await_phase(eff_at)
    rows = table[...].reshape(NV, TB)
    cols = jnp.concatenate([p.astype(F32) for p in pieces(rows)], axis=0).astype(BF16)
    hi3 = jnp.concatenate([oh_hi, oh_hi, oh_hi], axis=0).astype(BF16)
    picked = dot(cols, hi3, TN)
    ends = jnp.sum(jnp.where(oh_lo > 0, picked, 0.0), axis=0, keepdims=True)
    weight = ends[:, 0:BINS] * ends[:, BINS : 2 * BINS]
    back = back_ref[...]

    for k in range(SUBSETS):
        bins = slice(k * HALF, (k + 1) * HALF)
        w_k = weight[:, bins]
        rat_at, bck_at = [], []
        if k > 0:
            fwd_at = []
            for h in range(STREAMS):
                await_phase(img_at[h])
                total = jnp.zeros((FS, HALF), F32)
                for q in range(VQ):
                    quarter = img[h, q * NS : (q + 1) * NS].astype(F32).reshape(FS, VW).astype(BF16)
                    total = total + dot(quarter, a_ref[bins, q * VW : (q + 1) * VW], NT)
                fwd_send[h] = total.reshape(NS, FPART, HALF).astype(BF16)
                fwd_at.append(new_phase(slabs_of(fwd.at[k, h])))
                to_slabs(fwd_at[h], lambda w: fwd_send.at[h, w], fwd.at[k, h, s])
                fwd[k, h, s] = fwd_send[h, s]
        for h in range(STREAMS):
            await_phase(fwd_at[h])
            summed = jnp.sum(fwd[k, h].astype(F32), axis=0)
            ratio = (w_k * meas[h][:, bins]) / (w_k * summed + back[:, bins])
            rat[k, h, s] = ratio.astype(BF16)
            rat_at.append(new_phase(slabs_of(rat.at[k, h])))
            to_slabs(rat_at[h], lambda w: rat.at[k, h, s], rat.at[k, h, s])

        if k == 0:
            row = lax.broadcasted_iota(jnp.int32, (16, BINS), 0)
            half = lax.broadcasted_iota(jnp.int32, (16, BINS), 1) // HALF
            lhs = jnp.where(row == half, jnp.broadcast_to(weight, (16, BINS)), 0.0).astype(BF16)
            both = dot(lhs, a_ref[...], NN)
            for q in range(VQ):
                sens_send[q] = both[0:SUBSETS, q * VW : (q + 1) * VW]
            sens_at = new_phase(views_of(sens))
            to_views(sens_at, lambda w: sens_send.at[lax.rem(w, VQ)], sens.at[v])
            sens[v] = sens_send[vi]

        for h in range(STREAMS):
            await_phase(rat_at[h])
            lhs = rat[k, h].astype(F32).reshape(FS, HALF).astype(BF16)
            for q in range(VQ):
                product = dot(lhs, a_ref[bins, q * VW : (q + 1) * VW], NN)
                bck_send[k, h, q] = product.reshape(NS, FPART, VW).astype(BF16)
            bck_at.append(new_phase(views_of(bck.at[k, h])))
            to_views(bck_at[h], lambda w: bck_send.at[k, h, lax.rem(w, VQ), part_of(w)], bck.at[k, h, v])
            bck[k, h, v] = bck_send[k, h, vi, fi]

        if k == 0:
            await_phase(sens_at)
            sens_sum = jnp.sum(sens[...], axis=0)
        img_at, halves = [], []
        for h in range(STREAMS):
            await_phase(bck_at[h])
            back_image = jnp.sum(bck[k, h].astype(F32), axis=0)
            est[h] = est[h] * (back_image + SMOOTH) / (sens_sum[k : k + 1, :] + SMOOTH)
            halves.append(est[h].astype(BF16))
            if k < SUBSETS - 1:
                img_send[h] = halves[h]
                img_at.append(new_phase(views_of(img.at[h])))
                to_views(img_at[h], lambda w: img_send.at[h], img.at[h, slot])
                img[h, slot] = halves[h]

    part_sum = jnp.sum(halves[0].astype(F32), axis=0, keepdims=True)
    for h in range(1, STREAMS):
        part_sum = part_sum + jnp.sum(halves[h].astype(F32), axis=0, keepdims=True)
    sum_send[...] = part_sum
    sum_at = new_phase(views_of(sums))
    to_views(sum_at, lambda w: sum_send, sums.at[v])
    sums[v] = part_sum
    partner = lax.rem(v + 16, NV)
    pairs_at, pair_copies = [], []
    for h in range(STREAMS):
        fin[h, slot // 2, z] = est[h]
        number = next(numbers)
        pair_copies.append(
            pltpu.make_async_remote_copy(
                src_ref=fin.at[h, slot // 2, z], dst_ref=fin.at[h, slot // 2, z],
                send_sem=send_sem.at[number], recv_sem=recv_sem.at[number],
                device_id=(partner, s), device_id_type=MESH,
            )
        )
        pair_copies[h].start()
    await_phase(sum_at)
    fin_at = []
    for h in range(STREAMS):
        pair_copies[h].wait_recv()
        fin_at.append(new_phase(fin.at[h, pl.ds(0, 15)]))

        @pl.loop(1, 16)
        def _(i):
            w = 16 * z + lax.rem(lax.rem(v, 16) + i, 16)
            pltpu.make_async_remote_copy(
                src_ref=fin.at[h, slot // 2], dst_ref=fin.at[h, slot // 2],
                send_sem=send_sem.at[fin_at[h]], recv_sem=recv_sem.at[fin_at[h]],
                device_id=(w, s), device_id_type=MESH,
            ).start()

    quarter = []
    for q in range(VQ):
        total = sums[q]
        for f in range(1, NS):
            total = total + sums[f * VQ + q]
        quarter.append(total)
    image_sum = jnp.concatenate(quarter, axis=1)
    row = lax.broadcasted_iota(jnp.int32, (16, VOX), 0)
    hi, mid, low = [jnp.broadcast_to(p.astype(F32), (16, VOX)) for p in pieces(image_sum)]
    lhs = jnp.where(row == 0, hi, jnp.where(row == 1, mid, jnp.where(row == 2, low, 0.0))).astype(BF16)
    bins_sum = jnp.sum(dot(lhs, a_ref[...], NT), axis=0, keepdims=True)
    q_send[...] = bins_sum
    q_at = new_phase(slabs_of(q_recv))
    to_slabs(q_at, lambda w: q_send, q_recv.at[s])
    q_recv[s] = bins_sum
    await_phase(q_at)
    final = jnp.sum(q_recv[...], axis=0)
    expected = weight * final + FR * back
    fan_exp = fan(jnp.concatenate([expected, expected], axis=1), oh_hi, oh_lo)
    fan_send[:, 1:2, :] = fan_exp.reshape(NV, 1, TB)
    fan_at = new_phase(views_of(fan_recv))
    to_views(fan_at, lambda w: fan_send.at[w], fan_recv.at[v])
    fan_recv[v] = fan_send[v]

    for h in range(STREAMS):
        await_phase(fin_at[h])
    for q in range(VQ):
        block = fin[:, q * 4 : (q + 1) * 4].reshape(FR, VW)
        out_ref[pl.ds(q * VW, VW), :] = block.T

    await_phase(fan_at)
    totals = jnp.sum(fan_recv[...], axis=0)
    gain = eff_ref[0] * (totals[0:1, :] + FAN_OFFSET) / (totals[1:2, :] + FAN_OFFSET)
    gain_ref[...] = gain[:, 0:OWN]
    for number, ref in sent:
        await_all(send_sem.at[number], ref)
    for copy in pair_copies:
        copy.wait_send()


PHASES = 5 + STREAMS * (4 * SUBSETS + 1)


def on_device(
    tiles, tile_bin, tile_vox, tile_count, subset, pairs, measured, background, image, efficiency
):
    smem = pl.BlockSpec(memory_space=SMEM)
    vmem = pl.BlockSpec(memory_space=VMEM)
    hbm = pl.BlockSpec(memory_space=pl.ANY)
    shape = jax.ShapeDtypeStruct
    dma = pltpu.SemaphoreType.DMA
    count = tiles.shape[2]
    image_out, gain = pl.pallas_call(
        exchange,
        out_shape=(VMEM((VOX, FR), F32), VMEM((1, OWN), F32)),
        in_specs=[smem, smem] + [vmem] * 5 + [hbm] * 3,
        out_specs=(vmem, vmem),
        scratch_shapes=[
            VMEM((BINS, VOX), BF16),
            VMEM((count, TB, TB), BF16),
            VMEM((count, TB, TB), F32),
            VMEM((1, TB), jnp.int32),
            VMEM((8, TB), jnp.int32),
            SMEM((8, TB), jnp.int32),
            VMEM((1, BINS), F32),
            VMEM((2, BINS), jnp.int32),
            VMEM((NB, TB, FR), F32),
            VMEM((NB, TB, FR), F32),
            VMEM((FR, VOX), F32),
            VMEM((FR, BINS), F32),
            VMEM((STREAMS, NS, FPART, HALF), BF16),
            VMEM((1, 1, TB), F32),
            VMEM((NV, 1, TB), F32),
            VMEM((STREAMS, NS, FPART, HALF), BF16),
            VMEM((SUBSETS, STREAMS, NS, FPART, HALF), BF16),
            VMEM((SUBSETS, STREAMS, NS, FPART, HALF), BF16),
            VMEM((VQ, SUBSETS, VW), F32),
            VMEM((NV, SUBSETS, VW), F32),
            VMEM((SUBSETS, STREAMS, VQ, NS, FPART, VW), BF16),
            VMEM((SUBSETS, STREAMS, NV, FPART, VW), BF16),
            VMEM((STREAMS, FPART, VW), BF16),
            VMEM((STREAMS, NV, FPART, VW), BF16),
            VMEM((1, VW), F32),
            VMEM((NV, 1, VW), F32),
            VMEM((STREAMS, NV // 2, 2, FPART, VW), F32),
            VMEM((1, BINS), F32),
            VMEM((NS, 1, BINS), F32),
            VMEM((NV, 2, TB), F32),
            VMEM((NV, 2, TB), F32),
            dma((PHASES,)),
            dma((PHASES,)),
            dma((4,)),
        ],
        compiler_params=pltpu.CompilerParams(collective_id=0, has_side_effects=True),
        name="exchange",
    )(
        tile_count,
        subset,
        tile_bin.reshape(1, count),
        tile_vox.reshape(1, count),
        pairs,
        background.reshape(1, BINS),
        efficiency.reshape(1, OWN),
        tiles.reshape(tiles.shape[2:]),
        image.reshape(NB, TB, FR),
        measured.reshape(NB, TB, FR),
    )
    return image_out, gain.reshape(OWN)


def solution(mesh):
    return jax.shard_map(
        on_device,
        mesh=mesh,
        in_specs=(
            P("view", "slab", None, None, None),
            P("view", "slab", None),
            P("view", "slab", None),
            P("view", "slab"),
            P("view"),
            P(None, "view"),
            P("view", None),
            P("view"),
            P("slab", None),
            P("view"),
        ),
        out_specs=(P("slab", None), P("view")),
        check_vma=False,
    )
```
